32 devices in a mesh: row: 8 (over z, core), col: 4 (over y, x).
Axes of the slice: x: 2, y: 2, z: 4, core: 2. Of those that a mesh axis runs over, the one named last changes fastest.
Arguments:
- tokens: bfloat16 [24576, 1152], P(('row', 'col')), may hold values from -6 to 6
- condition: bfloat16 [6, 1152], P(None, 'row'), may hold values from -6 to 6
- clip_large: int32 [6], replicated, may hold values from 0 to 1, as said below
- modulator: bfloat16 [1152, 6, 1152], P('row', None, 'col'), may hold values from -0.1875 to 0.1875
- offsets: bfloat16 [6, 1152], P(None, 'col'), may hold values from -3 to 3
- projector: bfloat16 [1152, 3, 1152], P('row', None, 'col'), may hold values from -0.1875 to 0.1875
- priors: bfloat16 [2, 1152], P(None, 'col'), may hold values from -3 to 3
- combiner: bfloat16 [1152, 1152], P('row', 'col'), may hold values from -1.5 to 1.5
- margins: bfloat16 [1152], replicated, may hold values from -3 to 3
- expander: bfloat16 [1152, 4608], P('row', 'col'), may hold values from -0.1875 to 0.1875
- thresholds: bfloat16 [4608], P('col'), may hold values from -3 to 3
- reducer: bfloat16 [1152, 4608], P('row', 'col'), may hold values from -0.09375 to 0.09375
- baseline: bfloat16 [1152], replicated, may hold values from -3 to 3
- cotangent: bfloat16 [24576, 1152], P(('row', 'col')), may hold values from -6 to 6
Outputs:
- result: bfloat16 [24576, 1152], P(('row', 'col'))
- tokens_grad: float32 [24576, 1152], P(('row', 'col'))
- condition_grad: float32 [6, 1152], P(None, 'row')
- modulator_grad: float32 [1152, 6, 1152], P('row', None, 'col')
- offsets_grad: float32 [6, 1152], P(None, 'col')
- projector_grad: float32 [1152, 3, 1152], P('row', None, 'col')
- priors_grad: float32 [2, 1152], P(None, 'col')
- combiner_grad: float32 [1152, 1152], P('row', 'col')
- margins_grad: float32 [1152], replicated
- expander_grad: float32 [1152, 4608], P('row', 'col')
- thresholds_grad: float32 [4608], P('col')
- reducer_grad: float32 [1152, 4608], P('row', 'col')
- baseline_grad: float32 [1152], replicated
The draws below stay inside these ranges and needn't reach their ends.
Inputs may be any that keep to these rules, and one draw needn't show every extreme that they name: `clip_large`: 1 where the clip's frames have 1024 patches, 0 where they have 256; both kinds occur in every draw.
All inputs are finite; a program needn't handle non-finite values.
Results may differ from the reference program's by a relative error of at most 0.023.
Values may be sent and summed in bfloat16 or wider, within the bound.
A program may use at most 384 MiB of HBM per device.

```python
from functools import partial
import jax
import jax.numpy as jnp
from jax import lax

D = 1152
HEADS = 16
HEAD_DIM = 72
FF = 4608
PATCH_SMALL = 256
PATCH_BIG = 1024
CLIP_TOK = 4096
TOKENS = 24576
CLIPS = 6


def draw_clip_large(key, part):
    key_one, key_two = jax.random.split(key)
    tosses = jax.random.randint(key_one, (CLIPS,), 0, 2, dtype=jnp.int32)
    anchor = jax.random.randint(key_two, (), 0, CLIPS, dtype=jnp.int32)
    places = jnp.arange(CLIPS, dtype=jnp.int32)
    return jnp.where(places == anchor, 1, jnp.where(places == (anchor + 1) % CLIPS, 0, tosses)).astype(jnp.int32)


def level_of(rng, dims, pieces, smallest, top_value):
    def one(axis_at, shards_of):
        draws = jax.random.uniform(jax.random.fold_in(jax.random.fold_in(rng, 6), axis_at), (shards_of,), jnp.float32, smallest / len(pieces), top_value / len(pieces))
        return jnp.repeat(jnp.exp(draws), dims[axis_at] // shards_of).reshape((-1,) + (1,) * (len(dims) - axis_at - 1))

    level = one(*pieces[0])
    for cut in pieces[1:]:
        level = level * one(*cut)
    return level


def gaussian(key, extent, width, most, shards=(), kind=jnp.bfloat16):
    result = jax.random.normal(key, extent, jnp.float32) * width
    if len(shards) > 0:
        result = level_of(key, extent, shards, -0.22, 0.18) * result
    return jnp.clip(result, min=-most, max=most).astype(kind)


def setup_inputs(seed: int = 0) -> dict:
    key_list = jax.random.split(jax.random.key(seed), 15)
    return {
        "tokens": gaussian(key_list[0], (TOKENS, D), 1.0, 6.0, ((0, 32),)),
        "condition": gaussian(key_list[1], (CLIPS, D), 1.0, 6.0, ((1, 8),)),
        "clip_large": draw_clip_large(jax.random.fold_in(key_list[14], 71), 0),
        "modulator": gaussian(key_list[3], (D, 6, D), D ** -0.5, 0.1875, ((0, 8), (2, 4))),
        "offsets": gaussian(key_list[4], (6, D), 0.5, 3.0, ((1, 4),)),
        "projector": gaussian(key_list[5], (D, 3, D), D ** -0.5, 0.1875, ((0, 8), (2, 4))),
        "priors": gaussian(key_list[6], (2, D), 0.5, 3.0, ((1, 4),)),
        "combiner": gaussian(key_list[7], (D, D), (max(D // 64, 1)) ** -0.5, 1.5, ((0, 8), (1, 4))),
        "margins": gaussian(key_list[8], (D,), 0.5, 3.0),
        "expander": gaussian(key_list[9], (D, FF), D ** -0.5, 0.1875, ((0, 8), (1, 4))),
        "thresholds": gaussian(key_list[10], (FF,), 0.5, 3.0, ((0, 4),)),
        "reducer": gaussian(key_list[11], (D, FF), FF ** -0.5, 0.09375, ((0, 8), (1, 4))),
        "baseline": gaussian(key_list[12], (D,), 0.5, 3.0),
        "cotangent": gaussian(key_list[13], (TOKENS, D), 1.0, 6.0, ((0, 32),)),
    }


HIGH = lax.Precision.HIGHEST
EPSILON = 1e-06
NEGATIVE = -1e+30

@jax.custom_vjp
def low(v):
    return lax.optimization_barrier(v.astype(jnp.bfloat16)).astype(jnp.float32)

@jax.custom_vjp
def low_back(v):
    return v

def low_keep(v):
    return (low(v), None)

def low_pass(kept, grad):
    return (grad,)

def back_keep(v):
    return (v, None)

def back_low(kept, grad):
    return (low(grad),)
low.defvjp(low_keep, low_pass)
low_back.defvjp(back_keep, back_low)

def normalize(values):
    center = values - lax.optimization_barrier(jnp.mean(values, axis=-1, keepdims=True))
    return center * lax.rsqrt(lax.optimization_barrier(jnp.mean(center * center, axis=-1, keepdims=True)) + EPSILON)

def frame_mask(large_flag, length):
    places = jnp.arange(length, dtype=jnp.int32)
    frames = jnp.where(large_flag > 0, 0, places // PATCH_SMALL)
    return frames[:, None] == frames[None, :]

def slot_attention(packed):
    queries, key_rows, values, large_flag = packed
    scores = low_back(jnp.einsum('qhe,khe->hqk', queries, key_rows, precision=HIGH) * HEAD_DIM ** (-0.5))
    allowed = frame_mask(large_flag, queries.shape[0])
    softmax_weights = low(jax.nn.softmax(jnp.where(allowed[None], scores, NEGATIVE), axis=-1))
    return jnp.einsum('hqk,khe->qhe', softmax_weights, values, precision=HIGH)

def clip_layer(weights, packed):
    projector, priors, combiner, margins, expander, thresholds, reducer, baseline = weights
    clip_rows, modulation, large_flag = packed
    hat_one = normalize(clip_rows)
    hidden_one = low(hat_one * (1.0 + modulation[1]) + modulation[0])
    bias_three = jnp.stack([priors[0], jnp.zeros_like(priors[0]), priors[1]])
    triple = low(low_back(jnp.einsum('td,djc->tjc', hidden_one, projector, precision=HIGH) + bias_three[None]))
    slot_count = CLIP_TOK // PATCH_BIG
    head_parts = triple.reshape(slot_count, PATCH_BIG, 3, HEADS, HEAD_DIM)
    slot_flags = jnp.full((slot_count,), large_flag, dtype=jnp.int32)
    mixed_heads = lax.map(jax.checkpoint(slot_attention), (head_parts[:, :, 0], head_parts[:, :, 1], head_parts[:, :, 2], slot_flags))
    mixed_heads = low(low_back(mixed_heads.reshape(CLIP_TOK, D)))
    branch_one = low_back(jnp.dot(mixed_heads, combiner.T, precision=HIGH)) + margins
    residual = clip_rows + modulation[2] * branch_one
    hat_two = normalize(low(residual))
    hidden_two = low(hat_two * (1.0 + modulation[4]) + modulation[3])
    pre_act = low_back(jnp.dot(hidden_two, expander, precision=HIGH) + thresholds)
    activation = low(jax.nn.gelu(pre_act, approximate=True))
    branch_two = low_back(jnp.dot(activation, reducer.T, precision=HIGH)) + baseline
    return residual + modulation[5] * branch_two

def forward(tokens, condition, modulator, offsets, projector, priors, combiner, margins, expander, thresholds, reducer, baseline, clip_large):
    activated = jax.nn.silu(condition)
    modulation = jnp.einsum('kd,djc->kjc', activated, modulator, precision=HIGH) + offsets[None]
    clip_tokens = tokens.reshape(CLIPS, CLIP_TOK, D)
    weights = (projector, priors, combiner, margins, expander, thresholds, reducer, baseline)
    outputs = lax.map(jax.checkpoint(partial(clip_layer, weights)), (clip_tokens, modulation, clip_large))
    return outputs.reshape(CLIPS * CLIP_TOK, D)

def reference(tokens, condition, clip_large, modulator, offsets, projector, priors, combiner, margins, expander, thresholds, reducer, baseline, cotangent):
    floats = tuple((values.astype(jnp.float32) for values in (tokens, condition, modulator, offsets, projector, priors, combiner, margins, expander, thresholds, reducer, baseline)))
    primal, pullback = jax.vjp(lambda *params: forward(*params, clip_large), *floats)
    gradients = pullback(cotangent.astype(jnp.float32))
    return (primal.astype(jnp.bfloat16), gradients[0], gradients[1], gradients[2], gradients[3], gradients[4], gradients[5], gradients[6], gradients[7], gradients[8], gradients[9], gradients[10], gradients[11])
```

```python
import functools

import jax
import jax.numpy as jnp
from jax import lax
from jax.experimental import pallas as pl
from jax.experimental.pallas import tpu as pltpu
from jax.sharding import PartitionSpec as P

HEAD_DIM = 72
PATCH_SMALL = 256
PATCH_BIG = 1024
CLIP_TOK = 4096


HIGH = lax.Precision.HIGHEST
EPSILON = 1e-06
NEGATIVE = -1e30


def spread(values):
    return lax.all_gather(values, "col", axis=0, tiled=True)


def collect(values):
    return lax.psum_scatter(
        values.astype(jnp.bfloat16), "col", scatter_dimension=0, tiled=True
    ).astype(jnp.float32)


def spread_grad(values):
    return lax.all_gather(values, "col", axis=0, tiled=True)


def collect_grad(values):
    return lax.psum_scatter(
        values.astype(jnp.bfloat16), "col", scatter_dimension=0, tiled=True
    ).astype(jnp.float32)


def normalize(values):
    center = values - jnp.mean(values, axis=-1, keepdims=True)
    scaled = lax.rsqrt(jnp.mean(center * center, axis=-1, keepdims=True) + EPSILON)
    return (center * scaled, scaled)


def norm_back(grad_hat, hat_own, scaled):
    first_mean = jnp.mean(grad_hat, axis=-1, keepdims=True)
    second_mean = jnp.mean(grad_hat * hat_own, axis=-1, keepdims=True)
    return scaled * (grad_hat - first_mean - hat_own * second_mean)


def gelu_tanh(values):
    return jax.nn.gelu(values, approximate=True)


def frame_mask(large_flag, length):
    places = jnp.arange(length, dtype=jnp.int32)
    frames = jnp.where(large_flag > 0, 0, places // PATCH_SMALL)
    return frames[:, None] == frames[None, :]


def attend_slot(packed):
    queries, key_rows, values, large_flag = packed
    scores = jnp.einsum(
        "qhe,khe->hqk", queries, key_rows, preferred_element_type=jnp.float32
    ) * HEAD_DIM ** (-0.5)
    allowed = frame_mask(large_flag, queries.shape[0])
    scores = jnp.where(allowed[None], scores, NEGATIVE)
    row_peak = jnp.max(scores, axis=-1, keepdims=True)
    exp_scores = jnp.exp(scores - row_peak)
    row_total = jnp.sum(exp_scores, axis=-1, keepdims=True)
    soft_low = (exp_scores / row_total).astype(jnp.bfloat16)
    mixed_heads = jnp.einsum("hqk,khe->qhe", soft_low, values, preferred_element_type=jnp.float32)
    return (mixed_heads.astype(jnp.bfloat16), (row_peak + jnp.log(row_total))[..., 0])


def attend_back(packed):
    queries, key_rows, values, grad_mixed, logsum, large_flag = packed
    scores = jnp.einsum(
        "qhe,khe->hqk", queries, key_rows, preferred_element_type=jnp.float32
    ) * HEAD_DIM ** (-0.5)
    allowed = frame_mask(large_flag, queries.shape[0])
    soft_full = jnp.where(allowed[None], jnp.exp(scores - logsum[..., None]), 0.0)
    soft_low = soft_full.astype(jnp.bfloat16)
    grad_values = jnp.einsum(
        "hqk,qhe->khe", soft_low, grad_mixed, preferred_element_type=jnp.float32
    )
    grad_soft = jnp.einsum("qhe,khe->hqk", grad_mixed, values, preferred_element_type=jnp.float32)
    row_dot = jnp.sum(soft_full * grad_soft, axis=-1, keepdims=True)
    grad_scores = (soft_full * (grad_soft - row_dot)).astype(jnp.bfloat16)
    grad_queries = jnp.einsum(
        "hqk,khe->qhe", grad_scores, key_rows, preferred_element_type=jnp.float32
    ) * HEAD_DIM ** (-0.5)
    grad_keys = jnp.einsum(
        "hqk,qhe->khe", grad_scores, queries, preferred_element_type=jnp.float32
    ) * HEAD_DIM ** (-0.5)
    return jnp.stack([grad_queries, grad_keys, grad_values], axis=1).astype(jnp.bfloat16)


def shards(
    tokens,
    condition,
    clip_large,
    modulator,
    offsets,
    projector,
    priors,
    combiner,
    margins,
    expander,
    thresholds,
    reducer,
    baseline,
    cotangent,
):
    columns = lax.axis_size("col")
    col_index = lax.axis_index("col")
    row_index = lax.axis_index("row")
    own_rows, full_width = tokens.shape
    tok_rows = own_rows * columns
    col_width = full_width // columns
    slot_len = PATCH_BIG
    slot_count = tok_rows // slot_len
    heads_local = col_width // HEAD_DIM
    clip_count = condition.shape[0]
    ff_local = thresholds.shape[0]
    priors_float = priors.astype(jnp.float32)
    margins_float = margins.astype(jnp.float32)
    thresholds_float = thresholds.astype(jnp.float32)
    baseline_float = baseline.astype(jnp.float32)
    full_proj, full_comb, full_expand, full_reduce = (
        lax.all_gather(projector, "row", axis=0, tiled=True),
        lax.all_gather(combiner, "row", axis=0, tiled=True),
        lax.all_gather(expander, "row", axis=0, tiled=True),
        lax.all_gather(reducer, "row", axis=0, tiled=True),
    )
    cond_float = condition.astype(jnp.float32)
    activated = jax.nn.silu(cond_float)
    modulator_float = modulator.astype(jnp.float32)
    partial_mods = jnp.einsum("kd,djc->kjc", activated, modulator_float, precision=HIGH)
    own_mods = lax.psum(partial_mods, "row") + offsets.astype(jnp.float32)[None]
    all_mods = lax.all_gather(own_mods, "col", axis=2, tiled=True)
    clip_range = jnp.arange(clip_count, dtype=jnp.int32)
    slot_global = row_index * slot_count + jnp.arange(slot_count, dtype=jnp.int32)
    slot_clip = slot_global // (CLIP_TOK // PATCH_BIG)
    choose = slot_clip[:, None] == clip_range[None, :]
    slot_picker = choose.astype(jnp.float32)
    slot_mods = jnp.einsum("sk,kjd->sjd", slot_picker, all_mods, precision=HIGH)
    slot_large = jnp.sum(jnp.where(choose, clip_large[None, :], 0), axis=1)
    own_start = row_index * tok_rows + col_index * own_rows
    own_clip = (own_start + jnp.arange(own_rows, dtype=jnp.int32)) // CLIP_TOK
    row_picker = (own_clip[:, None] == clip_range[None, :]).astype(jnp.float32)
    row_mods = jnp.einsum("tk,kjd->tjd", row_picker, all_mods, precision=HIGH)

    def own_part(values):
        flat = values.reshape(tok_rows, values.shape[-1])
        return lax.dynamic_slice_in_dim(flat, col_index * own_rows, own_rows, 0)

    def forward_pass(inputs):
        token_part, mods_slot, mods_row, weight_set = inputs
        proj_rows, comb_rows, expand_rows, reduce_rows = weight_set
        gathered = spread(token_part).astype(jnp.float32).reshape(slot_count, slot_len, full_width)
        hat_one, scale_one = normalize(gathered)
        hidden_one = (hat_one * (1.0 + mods_slot[:, None, 1]) + mods_slot[:, None, 0]).astype(
            jnp.bfloat16
        )
        bias_three = jnp.stack([priors_float[0], jnp.zeros_like(priors_float[0]), priors_float[1]])
        triple = jnp.einsum(
            "spd,djc->spjc", hidden_one, proj_rows, preferred_element_type=jnp.float32
        )
        triple = (triple + bias_three).astype(jnp.bfloat16)
        head_parts = triple.reshape(slot_count, slot_len, 3, heads_local, HEAD_DIM)
        mixed_heads, logsum = lax.map(
            attend_slot, (head_parts[:, :, 0], head_parts[:, :, 1], head_parts[:, :, 2], slot_large)
        )
        mixed_heads = mixed_heads.reshape(slot_count, slot_len, col_width)
        attn_part = jnp.einsum(
            "spc,dc->spd", mixed_heads, comb_rows, preferred_element_type=jnp.float32
        )
        branch_one = collect(attn_part.reshape(tok_rows, full_width)) + margins_float
        residual = token_part.astype(jnp.float32) + mods_row[:, 2] * branch_one
        gathered_two = spread(residual.astype(jnp.bfloat16)).astype(jnp.float32)
        hat_two, scale_two = normalize(gathered_two.reshape(slot_count, slot_len, full_width))
        hidden_two = (hat_two * (1.0 + mods_slot[:, None, 4]) + mods_slot[:, None, 3]).astype(
            jnp.bfloat16
        )
        pre_act = (
            jnp.einsum("spd,df->spf", hidden_two, expand_rows, preferred_element_type=jnp.float32)
            + thresholds_float
        )
        activation = gelu_tanh(pre_act).astype(jnp.bfloat16)
        mlp_part = jnp.einsum(
            "spf,df->spd", activation, reduce_rows, preferred_element_type=jnp.float32
        )
        branch_two = collect(mlp_part.reshape(tok_rows, full_width)) + baseline_float
        layer_out = residual + mods_row[:, 5] * branch_two
        stored = (
            hat_one,
            scale_one,
            hidden_one,
            head_parts,
            mixed_heads,
            logsum,
            branch_one,
            hat_two,
            scale_two,
            hidden_two,
            pre_act,
            activation,
            branch_two,
        )
        return (layer_out, stored)

    weight_set = (full_proj, full_comb, full_expand, full_reduce)
    layer_out, stored = forward_pass((tokens, slot_mods, row_mods, weight_set))
    inputs_again = lax.optimization_barrier((tokens, slot_mods, row_mods, weight_set))
    stored = forward_pass(inputs_again)[1]
    (
        hat_one,
        scale_one,
        hidden_one,
        head_parts,
        mixed_keep,
        logsum,
        branch_one,
        hat_two,
        scale_two,
        hidden_two,
        pre_act,
        activation,
        branch_two,
    ) = stored
    grad_final = cotangent.astype(jnp.float32)
    grad_branch_two = grad_final * row_mods[:, 5]
    grad_gate_two = grad_final * branch_two
    grad_baseline = jnp.sum(grad_branch_two, axis=0)
    grad_mlp = spread_grad(grad_branch_two.astype(jnp.bfloat16)).reshape(
        slot_count, slot_len, full_width
    )
    grad_act = jnp.einsum("spd,df->spf", grad_mlp, full_reduce, preferred_element_type=jnp.float32)
    reducer_full = jnp.einsum(
        "spd,spf->df", grad_mlp, activation, preferred_element_type=jnp.float32
    )
    grad_pre = jax.vjp(gelu_tanh, pre_act)[1](grad_act)[0].astype(jnp.bfloat16)
    grad_thresholds = jnp.sum(grad_pre.astype(jnp.float32), axis=(0, 1))
    expander_full = jnp.einsum(
        "spd,spf->df", hidden_two, grad_pre, preferred_element_type=jnp.float32
    )
    hidden_two_part = jnp.einsum(
        "spf,df->spd", grad_pre, full_expand, preferred_element_type=jnp.float32
    )
    grad_hidden_two = collect_grad(hidden_two_part.reshape(tok_rows, full_width))
    hat_two_own = own_part(hat_two)
    grad_scale_two = grad_hidden_two * hat_two_own
    grad_residual = grad_final + norm_back(
        grad_hidden_two * (1.0 + row_mods[:, 4]), hat_two_own, own_part(scale_two)
    )
    grad_branch_one = grad_residual * row_mods[:, 2]
    grad_gate_one = grad_residual * branch_one
    grad_margins = jnp.sum(grad_branch_one, axis=0)
    grad_attn = spread_grad(grad_branch_one.astype(jnp.bfloat16)).reshape(
        slot_count, slot_len, full_width
    )
    grad_mixed = jnp.einsum(
        "spd,dc->spc", grad_attn, full_comb, preferred_element_type=jnp.float32
    ).astype(jnp.bfloat16)
    combiner_full = jnp.einsum(
        "spd,spc->dc", grad_attn, mixed_keep, preferred_element_type=jnp.float32
    )
    grad_heads = grad_mixed.reshape(slot_count, slot_len, heads_local, HEAD_DIM)
    grad_triple = lax.map(
        attend_back,
        (
            head_parts[:, :, 0],
            head_parts[:, :, 1],
            head_parts[:, :, 2],
            grad_heads,
            logsum,
            slot_large,
        ),
    )
    grad_triple = grad_triple.reshape(slot_count, slot_len, 3, col_width)
    triple_sums = jnp.sum(grad_triple.astype(jnp.float32), axis=(0, 1))
    projector_full = jnp.einsum(
        "spd,spjc->djc", hidden_one, grad_triple, preferred_element_type=jnp.float32
    )
    hidden_one_part = jnp.einsum(
        "spjc,djc->spd", grad_triple, full_proj, preferred_element_type=jnp.float32
    )
    grad_hidden_one = collect_grad(hidden_one_part.reshape(tok_rows, full_width))
    hat_one_own = own_part(hat_one)
    grad_scale_one = grad_hidden_one * hat_one_own
    grad_input = grad_residual + norm_back(
        grad_hidden_one * (1.0 + row_mods[:, 1]), hat_one_own, own_part(scale_one)
    )
    row_grads = jnp.stack(
        [
            grad_hidden_one,
            grad_scale_one,
            grad_gate_one,
            grad_hidden_two,
            grad_scale_two,
            grad_gate_two,
        ],
        axis=1,
    )
    clip_grads = jnp.einsum("tk,tjd->kjd", row_picker, row_grads, precision=HIGH)
    priors_wide = lax.dynamic_update_slice_in_dim(
        jnp.zeros((2, full_width), jnp.float32),
        jnp.stack([triple_sums[0], triple_sums[2]]),
        col_index * col_width,
        1,
    )
    thresholds_wide = lax.dynamic_update_slice_in_dim(
        jnp.zeros((ff_local * columns,), jnp.float32), grad_thresholds, col_index * ff_local, 0
    )
    projector_grad, combiner_grad, expander_grad, reducer_grad = (
        lax.psum_scatter(
            projector_full.astype(jnp.bfloat16), "row", scatter_dimension=0, tiled=True
        ).astype(jnp.float32),
        lax.psum_scatter(
            combiner_full.astype(jnp.bfloat16), "row", scatter_dimension=0, tiled=True
        ).astype(jnp.float32),
        lax.psum_scatter(
            expander_full.astype(jnp.bfloat16), "row", scatter_dimension=0, tiled=True
        ).astype(jnp.float32),
        lax.psum_scatter(
            reducer_full.astype(jnp.bfloat16), "row", scatter_dimension=0, tiled=True
        ).astype(jnp.float32),
    )
    small_sums = lax.psum(
        (clip_grads, priors_wide, grad_margins, thresholds_wide, grad_baseline), ("row", "col")
    )
    mod_own = lax.dynamic_slice_in_dim(small_sums[0], col_index * col_width, col_width, 2)
    modulator_grad = jnp.einsum("kd,kjc->djc", activated, mod_own, precision=HIGH)
    offsets_grad = jnp.sum(mod_own, axis=0)
    activated_grad = lax.psum(
        jnp.einsum("kjc,djc->kd", mod_own, modulator_float, precision=HIGH), "col"
    )
    condition_grad = jax.vjp(jax.nn.silu, cond_float)[1](activated_grad)[0]
    priors_grad = lax.dynamic_slice_in_dim(small_sums[1], col_index * col_width, col_width, 1)
    thresholds_grad = lax.dynamic_slice_in_dim(small_sums[3], col_index * ff_local, ff_local, 0)
    result = layer_out.astype(jnp.bfloat16)
    return (
        result,
        grad_input,
        condition_grad,
        modulator_grad,
        offsets_grad,
        projector_grad,
        priors_grad,
        combiner_grad,
        small_sums[2],
        expander_grad,
        thresholds_grad,
        reducer_grad,
        small_sums[4],
    )


BF = jnp.bfloat16
F32 = jnp.float32
GROUP = 4
BLOCK = 256
HALF = 512
LOG2E = 1.4426950408889634
SCALE2 = HEAD_DIM ** (-0.5) * LOG2E
GELU_C = 0.7978845608028654
GELU_A = 0.044715


def swap(values, axis_name, bit):
    size = lax.axis_size(axis_name)
    return lax.ppermute(values, axis_name, [(i, i ^ bit) for i in range(size)])


def x_swap(values):
    return swap(values, "col", 1)


def y_swap(values):
    return swap(values, "col", 2)


def core_swap(values):
    return swap(values, "row", 1)


def ordered(bit, own, other, axis):
    low = jnp.where(bit == 0, own, other)
    high = jnp.where(bit == 0, other, own)
    return jnp.concatenate([low, high], axis=axis)


def dot_nt(left, right):
    return lax.dot_general(left, right, (((1,), (1,)), ((), ())), preferred_element_type=F32)


def dot_nn(left, right):
    return jnp.dot(left, right, preferred_element_type=F32)


def dot_tn(left, right):
    return lax.dot_general(left, right, (((0,), (0,)), ((), ())), preferred_element_type=F32)


def window(head, width):
    low = head * HEAD_DIM // 128 * 128
    return low, min(width, -(-(head + 1) * HEAD_DIM // 128) * 128)


def pick(values, head):
    width = values.shape[1]
    low, high = window(head, width)
    at = lax.broadcasted_iota(jnp.int32, (values.shape[0], high - low), 1) + low
    inside = (at >= head * HEAD_DIM) & (at < (head + 1) * HEAD_DIM)
    return jnp.where(inside, values[:, low:high], jnp.zeros((), values.dtype))


def widen(values, low, width):
    rows, have = values.shape
    parts = []
    if low:
        parts.append(jnp.zeros((rows, low), values.dtype))
    parts.append(values)
    if low + have < width:
        parts.append(jnp.zeros((rows, width - low - have), values.dtype))
    return jnp.concatenate(parts, axis=1) if len(parts) > 1 else values


def attend_kernel(first_row, blocks, far, flag, *refs):
    width = GROUP * HEAD_DIM
    pitch = -(-3 * width // 128) * 128
    if far:
        tri, other, mix_ref, lse_ref, keys, vals = refs
    else:
        tri, mix_ref, lse_ref, keys, vals = refs
    near = blocks * BLOCK
    total = keys.shape[0]
    large = flag[0] > 0
    for g in range(2):
        base = g * pitch
        rows = pl.ds(first_row, near)
        keys[0:near, :] = tri[rows, base : base + width]
        vals[0:near, :] = tri[rows, base + width : base + 2 * width]
        if far:
            keys[near:total, :] = other[:, (1 - g) * 2 * width : (1 - g) * 2 * width + width]
            vals[near:total, :] = other[:, (1 - g) * 2 * width + width : (2 - g) * 2 * width]

        def step(i, carry, g=g, base=base):
            out_rows = pl.ds(pl.multiple_of(i * BLOCK, BLOCK), BLOCK)
            in_rows = pl.ds(pl.multiple_of(first_row + i * BLOCK, BLOCK), BLOCK)
            queries = tri[in_rows, base + 2 * width : base + 3 * width]

            def run(span):
                acc = None
                sums = []
                for h in range(GROUP):
                    low, high = window(h, width)
                    scores = dot_nt(pick(queries, h), keys[span, low:high])
                    peak = jnp.max(scores, axis=1, keepdims=True) * SCALE2
                    weights = jnp.exp2(scores * SCALE2 - peak)
                    denom = jnp.sum(weights, axis=1, keepdims=True)
                    part = dot_nn(weights.astype(BF), vals[span, low:high]) / denom
                    at = lax.broadcasted_iota(jnp.int32, part.shape, 1) + low
                    inside = (at >= h * HEAD_DIM) & (at < (h + 1) * HEAD_DIM)
                    part = widen(jnp.where(inside, part, 0.0), low, width)
                    acc = part if acc is None else acc + part
                    sums.append(jnp.broadcast_to(peak + jnp.log2(denom), (BLOCK, 32)))
                mix_ref[out_rows, g * width : (g + 1) * width] = acc.astype(BF)
                flipped = jnp.concatenate(sums, axis=1).T
                for h in range(GROUP):
                    lse_ref[g, i, h : h + 1, :] = flipped[32 * h : 32 * h + 1]

            @pl.when(large)
            def _():
                run(pl.ds(0, total))

            @pl.when(jnp.logical_not(large))
            def _():
                run(out_rows)

            return carry

        lax.fori_loop(0, blocks, step, 0)


def attend_fast(tri, flag, first_row, blocks, other=None):
    width = GROUP * HEAD_DIM
    far = other is not None
    total = blocks * BLOCK + (other.shape[0] if far else 0)
    rows = blocks * BLOCK
    in_vmem = pl.BlockSpec(memory_space=pltpu.VMEM)
    ins = [tri, other] if far else [tri]
    work = 2 * GROUP * rows * total
    return pl.pallas_call(
        functools.partial(attend_kernel, first_row, blocks, far),
        out_shape=(
            jax.ShapeDtypeStruct((rows, 2 * width), BF),
            jax.ShapeDtypeStruct((2, blocks, GROUP, BLOCK), F32),
        ),
        in_specs=[pl.BlockSpec(memory_space=pltpu.SMEM)] + [in_vmem] * len(ins),
        out_specs=(in_vmem, in_vmem),
        scratch_shapes=[pltpu.VMEM((total, width), BF)] * 2,
        cost_estimate=pl.CostEstimate(
            flops=work * 1024, bytes_accessed=8 * rows * 1024, transcendentals=work
        ),
        name="attend_far" if far else "attend_near",
    )(flag, *ins)


def attend_back_kernel(first_row, blocks, far, flag, *refs):
    width = GROUP * HEAD_DIM
    pitch = -(-3 * width // 128) * 128
    if far:
        tri, other, grad, mixed, lse, out, out_far = refs[:7]
        keys, vals, keys_t, grad_keys, grad_vals, grad_q = refs[7:]
    else:
        tri, grad, mixed, lse, out = refs[:5]
        keys, vals, keys_t, grad_keys, grad_vals, grad_q = refs[5:]
    near = blocks * BLOCK
    total = keys.shape[0]
    large = flag[0] > 0
    scale = HEAD_DIM ** (-0.5)
    for g in range(2):
        base = g * pitch
        rows = pl.ds(first_row, near)
        keys[0:near, :] = tri[rows, base : base + width]
        vals[0:near, :] = tri[rows, base + width : base + 2 * width]
        if far:
            keys[near:total, :] = other[:, (1 - g) * 2 * width : (1 - g) * 2 * width + width]
            vals[near:total, :] = other[:, (1 - g) * 2 * width + width : (2 - g) * 2 * width]
        for b in range(total // BLOCK):
            keys_t[:, b * BLOCK : (b + 1) * BLOCK] = keys[b * BLOCK : (b + 1) * BLOCK, :].T
        grad_keys[...] = jnp.zeros_like(grad_keys)
        grad_vals[...] = jnp.zeros_like(grad_vals)

        def step(i, carry, g=g, base=base):
            out_rows = pl.ds(pl.multiple_of(i * BLOCK, BLOCK), BLOCK)
            in_rows = pl.ds(pl.multiple_of(first_row + i * BLOCK, BLOCK), BLOCK)

            def run(span):
                queries = tri[in_rows, base + 2 * width : base + 3 * width]
                grad_mix = grad[in_rows, g * width : (g + 1) * width]
                mix = mixed[out_rows, g * width : (g + 1) * width]
                prod = (grad_mix.astype(F32) * mix.astype(F32)).T
                outs = []
                for h in range(GROUP):
                    low, high = window(h, width)
                    q_head = pick(queries, h)
                    g_head = pick(grad_mix, h)
                    dot_row = jnp.sum(
                        prod[h * HEAD_DIM : (h + 1) * HEAD_DIM], axis=0, keepdims=True
                    )
                    lse_row = lse[g, i, h : h + 1, :]
                    soft = jnp.exp2(dot_nt(keys[span, low:high], q_head) * SCALE2 - lse_row)
                    grad_soft = dot_nt(vals[span, low:high], g_head)
                    grad_scores = (soft * (grad_soft - dot_row)).astype(BF)
                    grad_vals[span, low:high] += dot_nn(soft.astype(BF), g_head)
                    grad_keys[span, low:high] += dot_nn(grad_scores, q_head)
                    top = h * HEAD_DIM // 16 * 16
                    end = -(-(h + 1) * HEAD_DIM // 16) * 16
                    part = dot_nn(keys_t[top:end, span], grad_scores)
                    outs.append(part[h * HEAD_DIM - top : h * HEAD_DIM - top + HEAD_DIM])
                grad_q[out_rows, :] = (jnp.concatenate(outs, axis=0) * scale).T.astype(BF)

            @pl.when(large)
            def _():
                run(pl.ds(0, total))

            @pl.when(jnp.logical_not(large))
            def _():
                run(out_rows)

            return carry

        lax.fori_loop(0, blocks, step, 0)
        pad = jnp.zeros((BLOCK, pitch - 3 * width), BF)
        for b in range(blocks):
            at = slice(b * BLOCK, (b + 1) * BLOCK)
            out[at, base : base + pitch] = jnp.concatenate(
                [
                    (grad_keys[at, :] * scale).astype(BF),
                    grad_vals[at, :].astype(BF),
                    grad_q[at, :],
                    pad,
                ],
                axis=1,
            )
        if far:
            out_far[:, g * 2 * width : (g + 1) * 2 * width] = jnp.concatenate(
                [
                    (grad_keys[near:total, :] * scale).astype(BF),
                    grad_vals[near:total, :].astype(BF),
                ],
                axis=1,
            )


def attend_back_fast(tri, flag, first_row, blocks, grad, mixed, lse, other=None):
    width = GROUP * HEAD_DIM
    pitch = -(-3 * width // 128) * 128
    far = other is not None
    rows = blocks * BLOCK
    total = rows + (other.shape[0] if far else 0)
    in_vmem = pl.BlockSpec(memory_space=pltpu.VMEM)
    ins = ([tri, other] if far else [tri]) + [grad, mixed, lse]
    outs = [jax.ShapeDtypeStruct((rows, 2 * pitch), BF)]
    if far:
        outs.append(jax.ShapeDtypeStruct((total - rows, 4 * width), BF))
    work = 2 * GROUP * rows * total
    return pl.pallas_call(
        functools.partial(attend_back_kernel, first_row, blocks, far),
        out_shape=tuple(outs),
        in_specs=[pl.BlockSpec(memory_space=pltpu.SMEM)] + [in_vmem] * len(ins),
        out_specs=tuple([in_vmem] * len(outs)),
        scratch_shapes=[
            pltpu.VMEM((total, width), BF),
            pltpu.VMEM((total, width), BF),
            pltpu.VMEM((width, total), BF),
            pltpu.VMEM((total, width), F32),
            pltpu.VMEM((total, width), F32),
            pltpu.VMEM((rows, width), BF),
        ],
        cost_estimate=pl.CostEstimate(
            flops=work * 2560, bytes_accessed=16 * rows * 1024, transcendentals=work
        ),
        name="attend_back_far" if far else "attend_back_near",
    )(flag, *ins)


def fast_shards(
    tokens,
    condition,
    clip_large,
    modulator,
    offsets,
    projector,
    priors,
    combiner,
    margins,
    expander,
    thresholds,
    reducer,
    baseline,
    cotangent,
):
    col = lax.axis_index("col")
    row = lax.axis_index("row")
    x_bit, y_bit = col % 2, col // 2
    core, z_low, z_high = row % 2, row // 2 % 2, row // 4
    own_rows, width = tokens.shape
    pair_rows = 2 * own_rows
    full_rows = PATCH_BIG
    col_width = width // 4
    pitch = -(-3 * col_width // 128) * 128
    clip_count = condition.shape[0]
    ff_local = thresholds.shape[0]
    per_clip = CLIP_TOK // PATCH_BIG
    blocks = pair_rows // BLOCK
    full_blocks = full_rows // BLOCK

    def canonical(own, other):
        wide = jnp.concatenate([own, other, own, other], axis=0)
        start = (HALF * y_bit + 2 * pair_rows - own_rows * x_bit) % pair_rows
        return lax.dynamic_slice_in_dim(wide, start, pair_rows, 0)

    def own_first(values):
        wide = jnp.concatenate([values, values], axis=0)
        start = (own_rows * x_bit + pair_rows - HALF * y_bit) % pair_rows
        return lax.dynamic_slice_in_dim(wide, start, pair_rows, 0)

    cond_float = condition.astype(F32)
    activated = jax.nn.silu(cond_float)
    modulator_float = modulator.astype(F32)
    mods = jnp.einsum("kd,djc->kjc", activated, modulator_float, precision=HIGH)
    for bit in (1, 2, 4):
        mods = mods + swap(mods, "row", bit)
    mods = (mods + offsets.astype(F32)[None])[:, :, None, :]
    mods = ordered(x_bit, mods, x_swap(mods), 2)
    mods = ordered(y_bit, mods, y_swap(mods), 2)
    all_mods = mods.reshape(clip_count, 6, width)

    tokens_far = x_swap(tokens)
    cot_in = lax.optimization_barrier((cotangent, tokens_far))[0]
    cot_far = x_swap(cot_in)
    pair_tokens = canonical(tokens, tokens_far)

    slot_full = row * 3 + 2 * y_bit
    slot_half = row * 3 + 1
    clip_full = slot_full // per_clip
    clip_half = slot_half // per_clip
    mods_full = lax.dynamic_index_in_dim(all_mods, clip_full, 0, False)
    mods_half = lax.dynamic_index_in_dim(all_mods, clip_half, 0, False)
    flag_full = lax.dynamic_slice_in_dim(clip_large, clip_full, 1, 0)
    flag_half = lax.dynamic_slice_in_dim(clip_large, clip_half, 1, 0)
    is_half = (jnp.arange(blocks) >= full_blocks)[:, None, None]

    def by_block(j):
        return jnp.where(is_half, mods_half[j][None, None], mods_full[j][None, None])

    own_block = (own_rows * x_bit + pair_rows - HALF * y_bit) % pair_rows // BLOCK
    own_ids = (own_block + jnp.arange(own_rows // BLOCK)) % blocks
    own_half = (own_ids >= full_blocks)[:, None, None]

    def own_by_block(j):
        return jnp.where(own_half, mods_half[j][None, None], mods_full[j][None, None])

    def split(values):
        return values.reshape(-1, BLOCK, values.shape[-1])

    def merge(values):
        return values.reshape(-1, values.shape[-1])

    def gather(shard):
        return lax.all_gather(shard, "row", axis=0, tiled=True)

    def fetch(values, exchange):
        rows = values.shape[0] // 2
        part = lax.dynamic_slice_in_dim(values, core * rows, rows, 0)
        part = exchange(part)
        return ordered(core, part, core_swap(part), 0)

    shard = jnp.concatenate(
        [
            projector[:, 1],
            projector[:, 2],
            projector[:, 0],
            jnp.zeros((projector.shape[0], pitch - 3 * col_width), BF),
        ],
        axis=1,
    )
    proj_own = gather(shard)
    comb_own = gather(combiner)
    expand_own = gather(expander)
    reduce_own = gather(reducer)
    proj = jnp.concatenate([proj_own, fetch(proj_own, y_swap)], axis=1)
    comb_near = jnp.concatenate([comb_own, fetch(comb_own, y_swap)], axis=1)
    comb = jnp.concatenate([comb_near, fetch(comb_near, x_swap)], axis=1)
    expand = jnp.concatenate([expand_own, fetch(expand_own, y_swap)], axis=1)
    reduce = jnp.concatenate([reduce_own, fetch(reduce_own, y_swap)], axis=1)
    priors_two = jnp.stack([priors, y_swap(priors)]).astype(F32)
    limits = jnp.concatenate([thresholds, y_swap(thresholds)]).astype(F32)
    bias = jnp.concatenate(
        [
            jnp.zeros((2, col_width), F32),
            priors_two[:, 1],
            priors_two[:, 0],
            jnp.zeros((2, pitch - 3 * col_width), F32),
        ],
        axis=1,
    ).reshape(1, 2 * pitch)

    hat_one, scale_one = normalize(split(pair_tokens.astype(F32)))
    hidden_one = merge((hat_one * (1.0 + by_block(1)) + by_block(0)).astype(BF))
    triple = (dot_nn(hidden_one, proj) + bias).astype(BF)
    kv_send = jnp.concatenate(
        [
            triple[full_rows:, : 2 * col_width],
            triple[full_rows:, pitch : pitch + 2 * col_width],
        ],
        axis=1,
    )
    kv_far = y_swap(kv_send)
    mix_full, lse_full = attend_fast(triple, flag_full, 0, full_blocks)
    mix_half, lse_half = attend_fast(
        triple, flag_half, full_rows, blocks - full_blocks, kv_far
    )
    mixed = jnp.concatenate(
        [
            jnp.concatenate([mix_full, x_swap(mix_full)], axis=1),
            jnp.concatenate([mix_half, x_swap(mix_half)], axis=1),
        ],
        axis=0,
    )
    branch_one = dot_nt(mixed, comb) + margins.astype(F32)
    residual = merge(
        split(pair_tokens.astype(F32)) + by_block(2) * split(branch_one)
    )
    hat_two, scale_two = normalize(split(residual.astype(BF).astype(F32)))
    hidden_two = merge((hat_two * (1.0 + by_block(4)) + by_block(3)).astype(BF))

    pair_cot = canonical(cotangent, cot_far).astype(F32)
    grad_mlp = merge((split(pair_cot) * by_block(5)).astype(BF))
    grad_act = dot_nn(grad_mlp, reduce)
    pre_act = dot_nn(hidden_two, expand) + limits
    inner = jnp.tanh(GELU_C * (pre_act + GELU_A * pre_act * pre_act * pre_act))
    activation = (0.5 * pre_act * (1.0 + inner)).astype(BF)
    slope = 0.5 * (1.0 + inner) + 0.5 * pre_act * (1.0 - inner * inner) * GELU_C * (
        1.0 + 3.0 * GELU_A * pre_act * pre_act
    )
    grad_pre = (grad_act * slope).astype(BF)
    grad_limits = jnp.sum(grad_pre.astype(F32), axis=0)
    back_two = own_first(dot_nt(grad_pre, expand).astype(BF))
    grad_hidden_two = back_two[:own_rows].astype(F32) + x_swap(back_two[own_rows:]).astype(F32)
    mlp_out = own_first(dot_nt(activation, reduce).astype(BF))
    branch_two = (
        mlp_out[:own_rows].astype(F32)
        + x_swap(mlp_out[own_rows:]).astype(F32)
        + baseline.astype(F32)
    )
    reduce_grad = dot_tn(grad_mlp, activation).astype(BF)
    expand_grad = dot_tn(hidden_two, grad_pre).astype(BF)

    residual_own = own_first(residual)[:own_rows]
    cot_own = cotangent.astype(F32)
    result = merge(
        split(residual_own) + own_by_block(5) * split(branch_two)
    ).astype(BF)
    hat_two_own = own_first(merge(hat_two).astype(BF))[:own_rows].astype(F32)
    scale_two_own = own_first(scale_two.reshape(pair_rows, 1))[:own_rows]
    branch_one_own = own_first(branch_one)[:own_rows]
    grad_residual = cot_own + norm_back(
        merge(split(grad_hidden_two) * (1.0 + own_by_block(4))), hat_two_own, scale_two_own
    )
    grad_one = merge(split(grad_residual) * own_by_block(2))
    grad_attn = grad_one.astype(BF)
    grad_mixed = dot_nn(grad_attn, comb).astype(BF)
    grad_mixed_far = x_swap(grad_mixed[:, 2 * col_width :])
    grad_mix = canonical(grad_mixed[:, : 2 * col_width], grad_mixed_far)
    mixed_own = own_first(mixed)[:own_rows]
    comb_grad = dot_tn(grad_attn, mixed_own).astype(BF)

    back_half, back_far = attend_back_fast(
        triple,
        flag_half,
        full_rows,
        blocks - full_blocks,
        grad_mix,
        mix_half,
        lse_half,
        kv_far,
    )
    (back_full,) = attend_back_fast(
        triple, flag_full, 0, full_blocks, grad_mix, mix_full, lse_full
    )
    back_got = y_swap(back_far)
    gap = jnp.zeros((HALF, pitch - 2 * col_width), F32)
    back_add = jnp.concatenate(
        [
            back_got[:, 2 * col_width :].astype(F32),
            gap,
            back_got[:, : 2 * col_width].astype(F32),
            gap,
        ],
        axis=1,
    )
    back_half = (back_half.astype(F32) + back_add).astype(BF)
    grad_triple = jnp.concatenate([back_full, back_half], axis=0)
    triple_sums = jnp.sum(grad_triple.astype(F32), axis=0).reshape(2, pitch)
    back_one = dot_nt(grad_triple, proj)
    sums_shift = jnp.sum(split(back_one), axis=1)
    sums_scale = jnp.sum(split(back_one) * hat_one, axis=1)
    back_one = own_first(back_one.astype(BF))
    grad_hidden_one = back_one[:own_rows].astype(F32) + x_swap(back_one[own_rows:]).astype(F32)
    proj_grad = dot_tn(hidden_one, grad_triple).astype(BF)
    hat_one_own, scale_one_own = normalize(split(tokens.astype(F32)))
    grad_input = grad_residual + norm_back(
        merge(split(grad_hidden_one) * (1.0 + own_by_block(1))),
        merge(hat_one_own),
        merge(scale_one_own),
    )

    def scatter(values, wide):
        cols = values.shape[1] // (4 if wide else 2)
        whole = values.reshape(4, 2, values.shape[0] // 8, values.shape[1])
        keep = lax.dynamic_index_in_dim(whole, core, 1, False)
        send = lax.dynamic_index_in_dim(whole, 1 - core, 1, False)
        keep = (keep.astype(F32) + core_swap(send).astype(F32)).astype(BF)
        if wide:
            got = x_swap(keep[:, :, 2 * cols :])
            keep = (keep[:, :, : 2 * cols].astype(F32) + got.astype(F32)).astype(BF)
        got = y_swap(keep[:, :, cols:])
        keep = (keep[:, :, :cols].astype(F32) + got.astype(F32)).astype(BF)
        keep = keep.reshape(2, 2, *keep.shape[1:])
        mine = lax.dynamic_index_in_dim(keep, z_high, 0, False)
        send = lax.dynamic_index_in_dim(keep, 1 - z_high, 0, False)
        keep = (mine.astype(F32) + swap(send, "row", 4).astype(F32)).astype(BF)
        mine = lax.dynamic_index_in_dim(keep, z_low, 0, False)
        send = lax.dynamic_index_in_dim(keep, 1 - z_low, 0, False)
        return mine.astype(F32) + swap(send, "row", 2).astype(F32)

    reducer_grad = scatter(reduce_grad, False)
    expander_grad = scatter(expand_grad, False)
    combiner_grad = scatter(comb_grad, True)
    proj_sum = scatter(proj_grad, False)
    projector_grad = jnp.stack(
        [
            proj_sum[:, 2 * col_width : 3 * col_width],
            proj_sum[:, :col_width],
            proj_sum[:, col_width : 2 * col_width],
        ],
        axis=1,
    )

    def total(values):
        for name, bit in (("row", 1), ("row", 2), ("col", 1), ("col", 2), ("row", 4)):
            values = values + swap(values, name, bit)
        return values

    clip_range = jnp.arange(clip_count, dtype=jnp.int32)
    pair_clip = jnp.where(jnp.arange(blocks) >= full_blocks, clip_half, clip_full)
    own_clip = jnp.where(own_ids >= full_blocks, clip_half, clip_full)
    pair_pick = (pair_clip[:, None] == clip_range[None]).astype(F32)
    own_pick = (own_clip[:, None] == clip_range[None]).astype(F32)

    def clip_sum(values, picker):
        return jnp.einsum("bk,bd->kd", picker, values, precision=HIGH)

    early = [
        clip_sum(jnp.sum(split(grad_residual * branch_one_own), axis=1), own_pick),
        clip_sum(jnp.sum(split(grad_hidden_two), axis=1), own_pick),
        clip_sum(jnp.sum(split(grad_hidden_two * hat_two_own), axis=1), own_pick),
        clip_sum(jnp.sum(split(cot_own * branch_two), axis=1), own_pick),
        jnp.sum(grad_one, axis=0)[None],
        jnp.sum(merge(split(cot_own) * own_by_block(5)), axis=0)[None],
    ]
    early = total(jnp.concatenate(early, axis=0))
    late = total(
        jnp.concatenate(
            [clip_sum(sums_shift, pair_pick), clip_sum(sums_scale, pair_pick)], axis=0
        )
    )
    rows_early = early[: 4 * clip_count].reshape(4, clip_count, width)
    rows_late = late.reshape(2, clip_count, width)
    grad_mods = jnp.concatenate([rows_late, rows_early], axis=0).transpose(1, 0, 2)
    mod_own = lax.dynamic_slice_in_dim(grad_mods, col * col_width, col_width, 2)
    modulator_grad = jnp.einsum("kd,kjc->djc", activated, mod_own, precision=HIGH)
    offsets_grad = jnp.sum(mod_own, axis=0)
    activated_grad = jnp.einsum("kjc,djc->kd", mod_own, modulator_float, precision=HIGH)
    activated_grad = activated_grad + x_swap(activated_grad)
    activated_grad = activated_grad + y_swap(activated_grad)
    condition_grad = jax.vjp(jax.nn.silu, cond_float)[1](activated_grad)[0]

    def fold(values):
        values = values[0] + y_swap(values[1])
        for bit in (1, 2, 4):
            values = values + swap(values, "row", bit)
        return values

    thresholds_grad = fold(grad_limits.reshape(2, ff_local))
    prior_sums = fold(triple_sums)
    priors_grad = jnp.stack(
        [prior_sums[2 * col_width : 3 * col_width], prior_sums[col_width : 2 * col_width]]
    )
    return (
        result,
        grad_input,
        condition_grad,
        modulator_grad,
        offsets_grad,
        projector_grad,
        priors_grad,
        combiner_grad,
        early[4 * clip_count],
        expander_grad,
        thresholds_grad,
        reducer_grad,
        early[4 * clip_count + 1],
    )


def solution(mesh):
    placed = (
        P(("row", "col"), None),
        P(None, "row"),
        P(),
        P("row", None, "col"),
        P(None, "col"),
        P("row", None, "col"),
        P(None, "col"),
        P("row", "col"),
        P(),
        P("row", "col"),
        P("col"),
        P("row", "col"),
        P(),
        P(("row", "col"), None),
    )
    fits = mesh.shape["row"] == 8 and mesh.shape["col"] == 4
    return jax.shard_map(
        fast_shards if fits else shards,
        mesh=mesh,
        in_specs=placed,
        out_specs=(
            P(("row", "col"), None),
            P(("row", "col"), None),
            P(None, "row"),
            P("row", None, "col"),
            P(None, "col"),
            P("row", None, "col"),
            P(None, "col"),
            P("row", "col"),
            P(),
            P("row", "col"),
            P("col"),
            P("row", "col"),
            P(),
        ),
        check_vma=False,
    )
```
